32 devices in a mesh: seq: 8 (over z, x), fsdp: 4 (over y, core).
Axes of the slice: x: 2, y: 2, z: 4, core: 2. Of those that a mesh axis runs over, the one named last changes fastest.
Arguments:
- inputs: bfloat16 [4, 1024, 768], P('fsdp', 'seq'), may hold values from -6 to 6
- cotangent: bfloat16 [4, 1024, 768], P('fsdp', 'seq'), may hold values from -6 to 6
- inproj: bfloat16 [1, 768, 3352], P(None, 'fsdp'), may hold values from -0.21875 to 0.21875
- outproj: bfloat16 [1, 1536, 768], P(None, 'fsdp'), may hold values from -0.15625 to 0.15625
- norm_gain: float32 [1, 768], replicated, may hold values from 0.5 to 2
- gate_gain: float32 [1, 1536], replicated, may hold values from 0.5 to 2
- conv_weight: float32 [1, 4, 1792], replicated, may hold values from -3 to 3
- conv_bias: float32 [1, 1792], replicated, may hold values from -0.5 to 0.5
- step_bias: float32 [1, 24], replicated, may hold values from -5.5 to -4.5
- log_rate: float32 [1, 24], replicated, may hold values from -7 to 1.5
- skip_gain: float32 [1, 24], replicated, may hold values from 0.5 to 2
Outputs:
- output: bfloat16 [4, 1024, 768], P('fsdp', 'seq')
- input_grad: bfloat16 [4, 1024, 768], P('fsdp', 'seq')
- inproj_grad: float32 [1, 768, 3352], P(None, 'fsdp')
- outproj_grad: float32 [1, 1536, 768], P(None, 'fsdp')
- norm_grad: float32 [1, 768], replicated
- gate_grad: float32 [1, 1536], replicated
- kernel_grad: float32 [1, 4, 1792], replicated
- bias_grad: float32 [1, 1792], replicated
- step_grad: float32 [1, 24], replicated
- rate_grad: float32 [1, 24], replicated
- skip_grad: float32 [1, 24], replicated
The draws below stay inside these ranges and needn't reach their ends.
All inputs are finite; a program needn't handle non-finite values.
Results may differ from the reference program's by a relative error of at most 0.01.
Values may be sent and summed in bfloat16 or wider, within the bound.
A program may use at most 192 MiB of HBM per device.

```python
import math
import jax
import jax.numpy as jnp
from jax import lax

D = 768
H = 24
P_SIZE = 64
N = 128
CONV = 4
SPAN = 64
LAYERS = 1
DI = 1536
XBC = 1792
F = 3352
LENGTH = 1024
SEQS = 4


def draw_log_rate(key, part):
    pick_key, slow_key, fast_key = jax.random.split(key, 3)
    slow_share = 0.5
    slow_mask = jax.random.bernoulli(pick_key, slow_share, (LAYERS, H))
    budget = jax.random.uniform(slow_key, (LAYERS, H), jnp.float32, 0.3, 2.0)
    slow_value = jnp.log(budget / (LENGTH * 0.011))
    fast_value = jax.random.uniform(fast_key, (LAYERS, H), jnp.float32, 0.5, 1.5)
    return jnp.where(slow_mask, slow_value, fast_value)


def levels(own_key, extent, cuts, least, top_value):
    def one(position, shards_of):
        draws = jax.random.uniform(jax.random.fold_in(jax.random.fold_in(own_key, 6), position), (shards_of,), jnp.float32, least / len(cuts), top_value / len(cuts))
        return jnp.repeat(jnp.exp(draws), extent[position] // shards_of).reshape((-1,) + (1,) * (len(extent) - position - 1))

    loudness = one(*cuts[0])
    for cut in cuts[1:]:
        loudness = loudness * one(*cut)
    return loudness


def bell_draw(stream_key, extent, spread, limit, shards=(), dtype=jnp.bfloat16):
    entries = jax.random.normal(stream_key, extent, jnp.float32) * spread
    if len(shards) > 0:
        entries = levels(stream_key, extent, shards, -0.22, 0.18) * entries
    return jnp.clip(entries, min=-limit, max=limit).astype(dtype)


def setup_inputs(seed: int = 0) -> dict:
    arg_keys = jax.random.split(jax.random.key(seed), 12)
    inputs = bell_draw(arg_keys[0], (SEQS, LENGTH, D), 1.0, 6.0, ((0, 4), (1, 8)))
    cotangent = bell_draw(arg_keys[1], (SEQS, LENGTH, D), 1.0, 6.0, ((0, 4), (1, 8)))
    inproj = bell_draw(arg_keys[2], (LAYERS, D, F), D ** -0.5, 0.21875, ((1, 4),))
    outproj = bell_draw(arg_keys[3], (LAYERS, DI, D), DI ** -0.5, 0.15625, ((1, 4),))
    norm_gain = jnp.clip(jnp.exp(jax.random.uniform(arg_keys[4], (LAYERS, D), jnp.float32, math.log(0.5), math.log(2.0))), 0.5, 2.0)
    gate_gain = jnp.clip(jnp.exp(jax.random.uniform(arg_keys[5], (LAYERS, DI), jnp.float32, math.log(0.5), math.log(2.0))), 0.5, 2.0)
    conv_weight = bell_draw(arg_keys[6], (LAYERS, CONV, XBC), CONV ** -0.5, 3.0, (), jnp.float32)
    conv_bias = jnp.clip(jax.random.uniform(arg_keys[7], (LAYERS, XBC), jnp.float32, -0.5, 0.5), -0.5, 0.5)
    step_bias = jnp.clip(jax.random.uniform(arg_keys[8], (LAYERS, H), jnp.float32, -5.5, -4.5), -5.5, -4.5)
    log_rate = draw_log_rate(jax.random.fold_in(arg_keys[11], 71), 0)
    skip_gain = jnp.clip(jnp.exp(jax.random.uniform(arg_keys[10], (LAYERS, H), jnp.float32, math.log(0.5), math.log(2.0))), 0.5, 2.0)
    return dict(inputs=inputs, cotangent=cotangent, inproj=inproj, outproj=outproj, norm_gain=norm_gain, gate_gain=gate_gain, conv_weight=conv_weight, conv_bias=conv_bias, step_bias=step_bias, log_rate=log_rate, skip_gain=skip_gain)


epsilon = 1e-05
highest = lax.Precision.HIGHEST

def rms_scale(values, gain):
    return values * lax.rsqrt(lax.optimization_barrier(jnp.mean(values * values, axis=-1, keepdims=True)) + epsilon) * gain

def section_one(projected, rim_rows, conv_weight, conv_bias, step_bias, log_rate):
    tokens = projected.shape[0]
    conv_input = projected[:, DI:DI + XBC]
    step_raw = projected[:, DI + XBC:]
    extended = jnp.concatenate([rim_rows, conv_input], axis=0)
    conv_sum = conv_bias + conv_weight[0] * extended[0:tokens]
    for offset in range(1, CONV):
        conv_sum = conv_sum + conv_weight[offset] * extended[offset:offset + tokens]
    conv_act = jax.nn.silu(conv_sum)
    blocks = tokens // SPAN
    head_input = conv_act[:, :DI].reshape(blocks, SPAN, H, P_SIZE)
    in_coeff = conv_act[:, DI:DI + N].reshape(blocks, SPAN, N)
    out_coeff = conv_act[:, DI + N:].reshape(blocks, SPAN, N)
    step_size = jax.nn.softplus(step_raw + step_bias).reshape(blocks, SPAN, H)
    decays = -jnp.exp(log_rate) * step_size
    inside = jnp.cumsum(decays, axis=1)
    inside_heads = jnp.swapaxes(inside, 1, 2)
    step_heads = jnp.swapaxes(step_size, 1, 2)
    scores = jnp.einsum('ktn,ksn->kts', out_coeff, in_coeff, precision=highest)
    log_gaps = inside_heads[:, :, :, None] - inside_heads[:, :, None, :]
    causal = jnp.arange(SPAN)[:, None] >= jnp.arange(SPAN)[None, :]
    decay_mat = jnp.exp(jnp.where(causal[None, None], log_gaps, -jnp.inf))
    decay_mat = decay_mat * scores[:, None] * step_heads[:, :, None, :]
    inner_out = jnp.einsum('khts,kshp->kthp', decay_mat, head_input, precision=highest)
    last_log = inside[:, -1:, :]
    tail_weight = jnp.exp(last_log - inside) * step_size
    span_state = jnp.einsum('ksh,kshp,ksn->khpn', tail_weight, head_input, in_coeff, precision=highest)
    totals = last_log[:, 0, :]

    def carry_step(carry_state, block_item):
        block_total, block_state = block_item
        return (jnp.exp(block_total)[:, None, None] * carry_state + block_state, carry_state)
    final_state, entering = lax.scan(carry_step, jnp.zeros((H, P_SIZE, N), jnp.float32), (totals, span_state))
    cross_out = jnp.einsum('kth,ktn,khpn->kthp', jnp.exp(inside), out_coeff, entering, precision=highest)
    offsets = jnp.cumsum(totals, axis=0) - totals
    cumulative = (inside + offsets[:, None, :]).reshape(tokens, H)
    ssm_zero = (inner_out + cross_out).reshape(tokens, H, P_SIZE)
    return (ssm_zero, cumulative, out_coeff.reshape(tokens, N), head_input.reshape(tokens, H, P_SIZE), final_state)

def section_two(projected, ssm_zero, cumulative, out_coeff, head_input, state_in, skip_gain, gate_gain):
    tokens = projected.shape[0]
    gate_part = projected[:, :DI]
    entering = jnp.einsum('tn,hpn->thp', out_coeff, state_in, precision=highest)
    ssm_full = ssm_zero + jnp.exp(cumulative)[:, :, None] * entering + skip_gain[None, :, None] * head_input
    gated = ssm_full.reshape(tokens, DI) * jax.nn.silu(gate_part)
    return rms_scale(gated, gate_gain)

def mixer_full(projected, conv_weight, conv_bias, step_bias, log_rate, skip_gain, gate_gain):
    rim_rows = jnp.zeros((CONV - 1, XBC), jnp.float32)
    ssm_zero, cumulative, out_coeff, head_input, final_state = section_one(projected, rim_rows, conv_weight, conv_bias, step_bias, log_rate)
    state_in = jnp.zeros((H, P_SIZE, N), jnp.float32)
    return section_two(projected, ssm_zero, cumulative, out_coeff, head_input, state_in, skip_gain, gate_gain)

def one_sequence(inputs, cotangent, inproj, outproj, norm_gain, gate_gain, conv_weight, conv_bias, step_bias, log_rate, skip_gain):
    stream = inputs.astype(jnp.float32)
    stored = []
    for layer_index in range(LAYERS):
        normed_f, pull_norm = jax.vjp(rms_scale, stream, norm_gain[layer_index])
        normed = normed_f.astype(jnp.bfloat16)
        projected = jnp.dot(normed, inproj[layer_index], preferred_element_type=jnp.float32)
        mixed_f, pull_mix = jax.vjp(mixer_full, projected, conv_weight[layer_index], conv_bias[layer_index], step_bias[layer_index], log_rate[layer_index], skip_gain[layer_index], gate_gain[layer_index])
        mixed_out = mixed_f.astype(jnp.bfloat16)
        stream = stream + jnp.dot(mixed_out, outproj[layer_index], preferred_element_type=jnp.float32)
        stored.append((normed, mixed_out, pull_norm, pull_mix))
    output = stream.astype(jnp.bfloat16)
    grad_stream = cotangent.astype(jnp.float32)
    grad_list = [None] * LAYERS
    for layer_index in reversed(range(LAYERS)):
        normed, mixed_out, pull_norm, pull_mix = stored[layer_index]
        out_grad = grad_stream.astype(jnp.bfloat16)
        mix_grad = jnp.dot(out_grad, outproj[layer_index].T, preferred_element_type=jnp.float32)
        outproj_term = jnp.dot(mixed_out.T, out_grad, preferred_element_type=jnp.float32)
        proj_grad, kernel_part, bias_part, step_part, rate_part, skip_part, gate_part = pull_mix(mix_grad)
        proj_grad_b = proj_grad.astype(jnp.bfloat16)
        normed_grad = jnp.dot(proj_grad_b, inproj[layer_index].T, preferred_element_type=jnp.float32)
        inproj_term = jnp.dot(normed.T, proj_grad_b, preferred_element_type=jnp.float32)
        stream_part, norm_part = pull_norm(normed_grad)
        grad_stream = grad_stream + stream_part
        grad_list[layer_index] = (inproj_term, outproj_term, norm_part, gate_part, kernel_part, bias_part, step_part, rate_part, skip_part)
    stacked = tuple((jnp.stack([entry[member] for entry in grad_list]) for member in range(9)))
    return (output, grad_stream.astype(jnp.bfloat16)) + stacked

def reference(inputs, cotangent, inproj, outproj, norm_gain, gate_gain, conv_weight, conv_bias, step_bias, log_rate, skip_gain):

    def per_sequence(sequence_pair):
        return one_sequence(sequence_pair[0], sequence_pair[1], inproj, outproj, norm_gain, gate_gain, conv_weight, conv_bias, step_bias, log_rate, skip_gain)
    results = lax.map(per_sequence, (inputs, cotangent))
    return (results[0], results[1], lax.optimization_barrier(jnp.sum(results[2], axis=0)), lax.optimization_barrier(jnp.sum(results[3], axis=0)), lax.optimization_barrier(jnp.sum(results[4], axis=0)), lax.optimization_barrier(jnp.sum(results[5], axis=0)), lax.optimization_barrier(jnp.sum(results[6], axis=0)), lax.optimization_barrier(jnp.sum(results[7], axis=0)), lax.optimization_barrier(jnp.sum(results[8], axis=0)), lax.optimization_barrier(jnp.sum(results[9], axis=0)), lax.optimization_barrier(jnp.sum(results[10], axis=0)))
```

```python
import jax
import jax.numpy as jnp
from jax import lax
from jax.sharding import PartitionSpec as P

H = 24
P_SIZE = 64
N = 128
CONV = 4
SPAN = 64
LAYERS = 1
DI = 1536
XBC = 1792


epsilon = 1e-05
highest = lax.Precision.HIGHEST


def passed_along(shard, axis, by):
    length = lax.axis_size(axis)
    pairs = [(i, i + by) for i in range(length) if 0 <= i + by < length]
    return lax.ppermute(shard, axis, pairs)


def span_weights(totals, index, forward):
    length = totals.shape[0]
    source = jnp.arange(length)[:, None]
    middle = jnp.arange(length)[None, :]
    if forward:
        between = (middle > source) & (middle < index)
        reached = jnp.arange(length) < index
    else:
        between = (middle < source) & (middle > index)
        reached = jnp.arange(length) > index
    logs = jnp.sum(jnp.where(between[:, :, None], totals[None], 0.0), axis=1)
    return jnp.where(reached[:, None], jnp.exp(logs), 0.0)


def weighted(parts, weights):
    return jnp.sum(weights[:, :, None, None] * parts.astype(jnp.float32), axis=0)


def rms_scale(values, gain):
    return values * lax.rsqrt(jnp.mean(values * values, axis=-1, keepdims=True) + epsilon) * gain


def section_one(projected, rim_rows, conv_weight, conv_bias, step_bias, log_rate):
    tokens = projected.shape[0]
    conv_input = projected[:, DI : DI + XBC]
    step_raw = projected[:, DI + XBC :]
    extended = jnp.concatenate([rim_rows, conv_input], axis=0)
    conv_sum = conv_bias + conv_weight[0] * extended[0:tokens]
    for offset in range(1, CONV):
        conv_sum = conv_sum + conv_weight[offset] * extended[offset : offset + tokens]
    conv_act = jax.nn.silu(conv_sum)
    blocks = 1
    head_input = conv_act[:, :DI].reshape(blocks, tokens, H, P_SIZE)
    in_coeff = conv_act[:, DI : DI + N].reshape(blocks, tokens, N)
    out_coeff = conv_act[:, DI + N :].reshape(blocks, tokens, N)
    step_size = jax.nn.softplus(step_raw + step_bias).reshape(blocks, tokens, H)
    decays = -jnp.exp(log_rate) * step_size
    inside = jnp.cumsum(decays, axis=1)
    inside_heads = jnp.swapaxes(inside, 1, 2)
    step_heads = jnp.swapaxes(step_size, 1, 2)
    scores = jnp.einsum("ktn,ksn->kts", out_coeff, in_coeff, precision=highest)
    log_gaps = inside_heads[:, :, :, None] - inside_heads[:, :, None, :]
    causal = jnp.arange(tokens)[:, None] >= jnp.arange(tokens)[None, :]
    decay_mat = jnp.exp(jnp.where(causal[None, None], log_gaps, -jnp.inf))
    decay_mat = decay_mat * scores[:, None] * step_heads[:, :, None, :]
    inner_out = jnp.einsum("khts,kshp->kthp", decay_mat, head_input, precision=highest)
    last_log = inside[:, -1:, :]
    tail_weight = jnp.exp(last_log - inside) * step_size
    span_state = jnp.einsum(
        "ksh,kshp,ksn->khpn", tail_weight, head_input, in_coeff, precision=highest
    )

    final_state = span_state[0]
    cumulative = inside.reshape(tokens, H)
    ssm_zero = inner_out.reshape(tokens, H, P_SIZE)
    return (
        ssm_zero,
        cumulative,
        out_coeff.reshape(tokens, N),
        head_input.reshape(tokens, H, P_SIZE),
        final_state,
    )


def section_two(
    projected, ssm_zero, cumulative, out_coeff, head_input, state_in, skip_gain, gate_gain
):
    tokens = projected.shape[0]
    gate_part = projected[:, :DI]
    entering = jnp.einsum("tn,hpn->thp", out_coeff, state_in, precision=highest)
    ssm_full = (
        ssm_zero
        + jnp.exp(cumulative)[:, :, None] * entering
        + skip_gain[None, :, None] * head_input
    )
    gated = ssm_full.reshape(tokens, DI) * jax.nn.silu(gate_part)
    return rms_scale(gated, gate_gain)


def on_device(
    inputs,
    cotangent,
    inproj,
    outproj,
    norm_gain,
    gate_gain,
    conv_weight,
    conv_bias,
    step_bias,
    log_rate,
    skip_gain,
):
    stream = inputs[0].astype(jnp.float32)
    tokens = stream.shape[0]
    rim = CONV - 1
    rim_start = tokens - rim
    index, shard = lax.axis_index("seq"), lax.axis_index("fsdp")
    inproj_full = lax.all_gather(inproj[0], "fsdp", axis=0, tiled=True)
    halo = passed_along(inputs[0, rim_start:], "seq", 1).astype(jnp.float32)
    normed_f, pull_norm = jax.vjp(rms_scale, stream, norm_gain[0])
    normed = normed_f.astype(jnp.bfloat16)
    halo_normed = rms_scale(halo, norm_gain[0]).astype(jnp.bfloat16)
    extra = jnp.pad(halo_normed, ((0, 8 - rim), (0, 0)))
    both = jnp.dot(
        jnp.concatenate([normed, extra], axis=0), inproj_full, preferred_element_type=jnp.float32
    )
    projected = both[:tokens]
    rim_rows = both[tokens : tokens + rim, DI : DI + XBC]
    outproj_full = lax.all_gather(outproj[0], "fsdp", axis=0, tiled=True)
    first_out, pull_first = jax.vjp(
        section_one, projected, rim_rows, conv_weight[0], conv_bias[0], step_bias[0], log_rate[0]
    )
    ssm_zero, cumulative, out_coeff, head_input, final_state = first_out
    total_log = cumulative[tokens - 1]
    totals = lax.all_gather(total_log, "seq")
    states = lax.all_gather(final_state.astype(jnp.bfloat16), "seq")
    state_in = weighted(states, span_weights(totals, index, True))
    mixed_f, pull_second = jax.vjp(
        section_two,
        projected,
        ssm_zero,
        cumulative,
        out_coeff,
        head_input,
        state_in,
        skip_gain[0],
        gate_gain[0],
    )
    mixed_out = mixed_f.astype(jnp.bfloat16)
    output = stream + jnp.dot(mixed_out, outproj_full, preferred_element_type=jnp.float32)
    out_grad = cotangent[0]
    mix_grad = jnp.dot(out_grad, outproj_full.T, preferred_element_type=jnp.float32)
    (
        proj_second,
        zero_grad,
        cum_part,
        coeff_grad,
        head_grad,
        state_grad,
        skip_part,
        gate_part,
    ) = pull_second(mix_grad)
    state_grads = lax.all_gather(state_grad.astype(jnp.bfloat16), "seq")
    later_grad = weighted(state_grads, span_weights(totals, index, False))
    total_grad = jnp.sum(later_grad * state_in, axis=(1, 2)) * jnp.exp(total_log)
    cum_grad = cum_part + jnp.pad(total_grad[None], ((tokens - 1, 0), (0, 0)))
    proj_first, rim_grad, kernel_part, bias_part, step_part, rate_part = pull_first(
        (zero_grad, cum_grad, coeff_grad, head_grad, later_grad)
    )
    rim_back = passed_along(rim_grad, "seq", -1)
    proj_grad = (
        proj_first
        + proj_second
        + jnp.pad(rim_back, ((rim_start, 0), (DI, projected.shape[1] - DI - XBC)))
    )
    proj_grad_b = proj_grad.astype(jnp.bfloat16)
    return finish(
        inputs, cotangent, inproj, outproj, stream, pull_norm, normed, mixed_out, output,
        inproj_full, proj_grad_b, shard,
        (gate_part, kernel_part, bias_part, step_part, rate_part, skip_part),
    )


def finish(
    inputs, cotangent, inproj, outproj, stream, pull_norm, normed, mixed_out, output,
    inproj_full, proj_grad_b, shard, parts,
):
    in_rows, out_rows = inproj.shape[1], outproj.shape[1]
    width = proj_grad_b.shape[1]
    grads_all = lax.all_gather(proj_grad_b, "fsdp")
    normed_all = lax.all_gather(normed.T, "fsdp")
    mixed_all = lax.all_gather(mixed_out.T, "fsdp")
    outer_all = lax.all_gather(cotangent[0], "fsdp")
    normed_own = lax.dynamic_slice_in_dim(normed_all, shard * in_rows, in_rows, 1)
    mixed_own = lax.dynamic_slice_in_dim(mixed_all, shard * out_rows, out_rows, 1)
    outproj_term = jnp.einsum("fkt,ftc->kc", mixed_own, outer_all, preferred_element_type=jnp.float32)
    normed_grad = jnp.dot(proj_grad_b, inproj_full.T, preferred_element_type=jnp.float32)
    stream_part, norm_part = pull_norm(normed_grad)
    grad_stream = cotangent[0].astype(jnp.float32) + stream_part
    small = [norm_part] + list(parts)
    sizes = [part.size for part in small]
    total = sum(sizes)
    rows = -(-total // width)
    lines = -(-total // 1024) * 8
    flat = jnp.concatenate([part.reshape(-1) for part in small] + [jnp.zeros((lines * 128 - total,), jnp.float32)])
    group = jnp.sum(lax.all_gather(flat.reshape(lines, 128), "fsdp"), axis=0).reshape(-1)
    group = jnp.pad(group[:total], (0, rows * width - total)).reshape(rows, width)
    inproj_term = jnp.einsum("fkt,ftc->kc", normed_own, grads_all, preferred_element_type=jnp.float32)
    joined = jnp.concatenate([inproj_term, group], axis=0).astype(jnp.bfloat16)
    joined_sum, outproj_sum = lax.psum((joined, outproj_term.astype(jnp.bfloat16)), "seq")
    inproj_grad = joined_sum[:in_rows].astype(jnp.float32)
    flat = joined_sum[in_rows:].astype(jnp.float32).reshape(-1)
    outs, at = [], 0
    for part, size in zip(small, sizes):
        outs.append(flat[at : at + size].reshape((1,) + part.shape))
        at += size
    return (
        output.astype(jnp.bfloat16)[None],
        grad_stream.astype(jnp.bfloat16)[None],
        inproj_grad[None],
        outproj_sum.astype(jnp.float32)[None],
        *outs,
    )


def solution(mesh):
    placed = (
        P("fsdp", "seq", None),
        P("fsdp", "seq", None),
        P(None, "fsdp", None),
        P(None, "fsdp", None),
        P(),
        P(),
        P(),
        P(),
        P(),
        P(),
        P(),
    )
    return jax.shard_map(
        on_device,
        mesh=mesh,
        in_specs=placed,
        out_specs=(
            P("fsdp", "seq", None),
            P("fsdp", "seq", None),
            P(None, "fsdp", None),
            P(None, "fsdp", None),
            P(),
            P(),
            P(),
            P(),
            P(),
            P(),
            P(),
        ),
        check_vma=False,
    )
```

```python
import jax
import jax.numpy as jnp
from jax import lax
from jax.sharding import PartitionSpec as P

H = 24
P_SIZE = 64
N = 128
CONV = 4
SPAN = 64
LAYERS = 1
DI = 1536
XBC = 1792


epsilon = 1e-05
highest = lax.Precision.HIGHEST


def passed_along(shard, axis, by):
    length = lax.axis_size(axis)
    pairs = [(i, i + by) for i in range(length) if 0 <= i + by < length]
    return lax.ppermute(shard, axis, pairs)


def swapped(shard, axis):
    pairs = [(i, i ^ 1) for i in range(lax.axis_size(axis))]
    return lax.ppermute(shard, axis, pairs)


def scaled(total, state):
    return jnp.exp(total)[:, None, None] * state


def handed_on(state, total, axis, sign):
    length = lax.axis_size(axis)
    odd = lax.axis_index(axis) % 2 == 1
    at_exit = odd if sign > 0 else jnp.logical_not(odd)
    half = state.shape[0] // 2

    def own_half(array):
        return jnp.where(odd, array[half:], array[:half])

    other = swapped(state.astype(jnp.bfloat16), axis).astype(jnp.float32)
    other_total = swapped(total, axis)
    out_state, in_state = jnp.where(at_exit, state, other), jnp.where(at_exit, other, state)
    out_total = jnp.where(at_exit, total, other_total)
    joint = own_half(out_state + scaled(out_total, in_state))
    joint_total = own_half(total + other_total)
    before, before_total = jnp.zeros_like(joint), jnp.zeros_like(joint_total)
    step = 1
    while step < length // 2:
        got = passed_along(joint.astype(jnp.bfloat16), axis, 2 * step * sign).astype(jnp.float32)
        got_total = passed_along(joint_total, axis, 2 * step * sign)
        before, before_total = before + scaled(before_total, got), before_total + got_total
        joint, joint_total = joint + scaled(joint_total, got), joint_total + got_total
        step *= 2
    rest = swapped(before.astype(jnp.bfloat16), axis).astype(jnp.float32)
    whole = jnp.where(
        odd, jnp.concatenate([rest, before], axis=0), jnp.concatenate([before, rest], axis=0)
    )
    return jnp.where(at_exit, other + scaled(other_total, whole), whole)


def rms_scale(values, gain):
    return values * lax.rsqrt(jnp.mean(values * values, axis=-1, keepdims=True) + epsilon) * gain


def section_one(projected, rim_rows, conv_weight, conv_bias, step_bias, log_rate):
    tokens = projected.shape[0]
    conv_input = projected[:, :XBC]
    step_raw = projected[:, XBC:]
    extended = jnp.concatenate([rim_rows, conv_input], axis=0)
    conv_sum = conv_bias + conv_weight[0] * extended[0:tokens]
    for offset in range(1, CONV):
        conv_sum = conv_sum + conv_weight[offset] * extended[offset : offset + tokens]
    conv_act = jax.nn.silu(conv_sum)
    blocks = 1
    head_input = conv_act[:, :DI].reshape(blocks, tokens, H, P_SIZE)
    in_coeff = conv_act[:, DI : DI + N].reshape(blocks, tokens, N)
    out_coeff = conv_act[:, DI + N :].reshape(blocks, tokens, N)
    step_size = jax.nn.softplus(step_raw + step_bias).reshape(blocks, tokens, H)
    decays = -jnp.exp(log_rate) * step_size
    inside = jnp.cumsum(decays, axis=1)
    inside_heads = jnp.swapaxes(inside, 1, 2)
    step_heads = jnp.swapaxes(step_size, 1, 2)
    scores = jnp.einsum("ktn,ksn->kts", out_coeff, in_coeff, precision=highest)
    log_gaps = inside_heads[:, :, :, None] - inside_heads[:, :, None, :]
    causal = jnp.arange(tokens)[:, None] >= jnp.arange(tokens)[None, :]
    decay_mat = jnp.exp(jnp.where(causal[None, None], log_gaps, -jnp.inf))
    decay_mat = decay_mat * scores[:, None] * step_heads[:, :, None, :]
    inner_out = jnp.einsum("khts,kshp->kthp", decay_mat, head_input, precision=highest)
    last_log = inside[:, -1:, :]
    tail_weight = jnp.exp(last_log - inside) * step_size
    span_state = jnp.einsum(
        "ksh,kshp,ksn->khpn", tail_weight, head_input, in_coeff, precision=highest
    )

    final_state = span_state[0]
    cumulative = inside.reshape(tokens, H)
    ssm_zero = inner_out.reshape(tokens, H, P_SIZE)
    return (
        ssm_zero,
        cumulative,
        out_coeff.reshape(tokens, N),
        head_input.reshape(tokens, H, P_SIZE),
        final_state,
    )


def section_two(
    gate_part, ssm_zero, cumulative, out_coeff, head_input, state_in, skip_gain, gate_gain
):
    tokens = gate_part.shape[0]
    entering = jnp.einsum("tn,hpn->thp", out_coeff, state_in, precision=highest)
    ssm_full = (
        ssm_zero
        + jnp.exp(cumulative)[:, :, None] * entering
        + skip_gain[None, :, None] * head_input
    )
    gated = ssm_full.reshape(tokens, DI) * jax.nn.silu(gate_part)
    return rms_scale(gated, gate_gain)


def by_owner(rows, columns):
    return jnp.einsum("ftk,ftc->kc", rows, columns, preferred_element_type=jnp.float32)


def on_device(
    inputs,
    cotangent,
    inproj,
    outproj,
    norm_gain,
    gate_gain,
    conv_weight,
    conv_bias,
    step_bias,
    log_rate,
    skip_gain,
):
    stream = inputs[0].astype(jnp.float32)
    tokens = stream.shape[0]
    rim = CONV - 1
    rim_start = tokens - rim
    index, shard = lax.axis_index("seq"), lax.axis_index("fsdp")
    rest_full = lax.all_gather(inproj[0, :, DI:], "fsdp", axis=0, tiled=True)
    halo = passed_along(inputs[0, rim_start:], "seq", 1).astype(jnp.float32)
    normed_f, pull_norm = jax.vjp(rms_scale, stream, norm_gain[0])
    normed = normed_f.astype(jnp.bfloat16)
    halo_normed = rms_scale(halo, norm_gain[0]).astype(jnp.bfloat16)
    extra = jnp.pad(halo_normed, ((0, 8 - rim), (0, 0)))
    both = jnp.dot(
        jnp.concatenate([normed, extra], axis=0), rest_full, preferred_element_type=jnp.float32
    )
    projected = both[:tokens]
    rim_rows = both[tokens : tokens + rim, :XBC]
    gate_full = lax.all_gather(inproj[0, :, :DI], "fsdp", axis=0, tiled=True)
    out_rows = outproj.shape[1]
    mixture = lax.all_gather(
        jnp.concatenate([outproj[0], cotangent[0], normed], axis=0), "fsdp"
    )
    outproj_full = mixture[:, :out_rows].reshape(-1, outproj.shape[2])
    outer_all = mixture[:, out_rows : out_rows + tokens]
    normed_own = lax.dynamic_slice_in_dim(
        mixture[:, out_rows + tokens :], shard * inproj.shape[1], inproj.shape[1], 2
    )
    projected_gate = jnp.dot(normed, gate_full, preferred_element_type=jnp.float32)
    first_out, pull_first = jax.vjp(
        section_one, projected, rim_rows, conv_weight[0], conv_bias[0], step_bias[0], log_rate[0]
    )
    ssm_zero, cumulative, out_coeff, head_input, final_state = first_out
    total_log = cumulative[tokens - 1]
    state_in = handed_on(final_state, total_log, "seq", 1)
    mixed_f, pull_second = jax.vjp(
        section_two,
        projected_gate,
        ssm_zero,
        cumulative,
        out_coeff,
        head_input,
        state_in,
        skip_gain[0],
        gate_gain[0],
    )
    mixed_out = mixed_f.astype(jnp.bfloat16)
    output = stream + jnp.dot(mixed_out, outproj_full, preferred_element_type=jnp.float32)
    out_grad = cotangent[0]
    mix_grad = jnp.dot(out_grad, outproj_full.T, preferred_element_type=jnp.float32)
    (
        gate_grad,
        zero_grad,
        cum_part,
        coeff_grad,
        head_grad,
        state_grad,
        skip_part,
        gate_part,
    ) = pull_second(mix_grad)
    later_grad = handed_on(state_grad, total_log, "seq", -1)
    mixed_all = lax.all_gather(mixed_out.T, "fsdp")
    mixed_own = lax.dynamic_slice_in_dim(mixed_all, shard * out_rows, out_rows, 1)
    gate_grad_b = gate_grad.astype(jnp.bfloat16)
    gate_all = lax.all_gather(gate_grad_b, "fsdp")
    outproj_term = jnp.einsum(
        "fkt,ftc->kc", mixed_own, outer_all, preferred_element_type=jnp.float32
    ).astype(jnp.bfloat16)
    gate_term = by_owner(normed_own, gate_all).astype(jnp.bfloat16)
    outproj_sum, gate_sum = lax.psum((outproj_term, gate_term), "seq")
    later_grad, outproj_term, gate_term = lax.optimization_barrier(
        (later_grad, outproj_term, gate_term)
    )
    total_grad = jnp.sum(later_grad * state_in, axis=(1, 2)) * jnp.exp(total_log)
    cum_grad = cum_part + jnp.pad(total_grad[None], ((tokens - 1, 0), (0, 0)))
    proj_first, rim_grad, kernel_part, bias_part, step_part, rate_part = pull_first(
        (zero_grad, cum_grad, coeff_grad, head_grad, later_grad)
    )
    rim_back = passed_along(rim_grad, "seq", -1)
    rest_grad = proj_first + jnp.pad(
        rim_back, ((rim_start, 0), (0, projected.shape[1] - XBC))
    )
    rest_grad_b = rest_grad.astype(jnp.bfloat16)
    rest_sent, outproj_sum, gate_sum = lax.optimization_barrier(
        (rest_grad_b, outproj_sum, gate_sum)
    )
    rest_all = lax.all_gather(rest_sent, "fsdp")
    contract = (((1,), (1,)), ((), ()))
    normed_grad = lax.dot_general(
        gate_grad_b, gate_full, contract, preferred_element_type=jnp.float32
    ) + lax.dot_general(rest_grad_b, rest_full, contract, preferred_element_type=jnp.float32)
    stream_part, norm_part = pull_norm(normed_grad)
    grad_stream = cotangent[0].astype(jnp.float32) + stream_part
    in_rows = inproj.shape[1]
    width = rest_grad_b.shape[1]
    small = [norm_part, gate_part, kernel_part, bias_part, step_part, rate_part, skip_part]
    sizes = [part.size for part in small]
    total = sum(sizes)
    rows = -(-total // width)
    lines = -(-total // 1024) * 8
    flat = jnp.concatenate([part.reshape(-1) for part in small] + [jnp.zeros((lines * 128 - total,), jnp.float32)])
    group = jnp.sum(lax.all_gather(flat.reshape(lines, 128), "fsdp"), axis=0).reshape(-1)
    group = jnp.pad(group[:total], (0, rows * width - total)).reshape(rows, width)
    rest_term = by_owner(normed_own, rest_all)
    joined = jnp.concatenate([rest_term, group], axis=0).astype(jnp.bfloat16)
    joined_sum = lax.psum(joined, "seq")
    inproj_grad = jnp.concatenate([gate_sum, joined_sum[:in_rows]], axis=1).astype(jnp.float32)
    flat = joined_sum[in_rows:].astype(jnp.float32).reshape(-1)
    outs, at = [], 0
    for part, size in zip(small, sizes):
        outs.append(flat[at : at + size].reshape((1,) + part.shape))
        at += size
    return (
        output.astype(jnp.bfloat16)[None],
        grad_stream.astype(jnp.bfloat16)[None],
        inproj_grad[None],
        outproj_sum.astype(jnp.float32)[None],
        *outs,
    )


def solution(mesh):
    placed = (
        P("fsdp", "seq", None),
        P("fsdp", "seq", None),
        P(None, "fsdp", None),
        P(None, "fsdp", None),
        P(),
        P(),
        P(),
        P(),
        P(),
        P(),
        P(),
    )
    return jax.shard_map(
        on_device,
        mesh=mesh,
        in_specs=placed,
        out_specs=(
            P("fsdp", "seq", None),
            P("fsdp", "seq", None),
            P(None, "fsdp", None),
            P(None, "fsdp", None),
            P(),
            P(),
            P(),
            P(),
            P(),
            P(),
            P(),
        ),
        check_vma=False,
    )
```

```python
import jax
import jax.numpy as jnp
from jax import lax
from jax.sharding import PartitionSpec as P

H = 24
P_SIZE = 64
N = 128
CONV = 4
SPAN = 64
LAYERS = 1
DI = 1536
XBC = 1792


epsilon = 1e-05
highest = lax.Precision.HIGHEST


def passed_along(shard, axis, by):
    length = lax.axis_size(axis)
    pairs = [(i, i + by) for i in range(length) if 0 <= i + by < length]
    return lax.ppermute(shard, axis, pairs)


def swapped(shard, axis):
    pairs = [(i, i ^ 1) for i in range(lax.axis_size(axis))]
    return lax.ppermute(shard, axis, pairs)


def scaled(total, state):
    return jnp.exp(total)[:, None, None] * state


def handed_on(state, total, axis, sign):
    length = lax.axis_size(axis)
    odd = lax.axis_index(axis) % 2 == 1
    at_exit = odd if sign > 0 else jnp.logical_not(odd)
    half = state.shape[0] // 2

    def own_half(array):
        return jnp.where(odd, array[half:], array[:half])

    other = swapped(state.astype(jnp.bfloat16), axis).astype(jnp.float32)
    other_total = swapped(total, axis)
    out_state, in_state = jnp.where(at_exit, state, other), jnp.where(at_exit, other, state)
    out_total = jnp.where(at_exit, total, other_total)
    joint = own_half(out_state + scaled(out_total, in_state))
    joint_total = own_half(total + other_total)
    before, before_total = jnp.zeros_like(joint), jnp.zeros_like(joint_total)
    step = 1
    while step < length // 2:
        got = passed_along(joint.astype(jnp.bfloat16), axis, 2 * step * sign).astype(jnp.float32)
        got_total = passed_along(joint_total, axis, 2 * step * sign)
        before, before_total = before + scaled(before_total, got), before_total + got_total
        joint, joint_total = joint + scaled(joint_total, got), joint_total + got_total
        step *= 2
    rest = swapped(before.astype(jnp.bfloat16), axis).astype(jnp.float32)
    whole = jnp.where(
        odd, jnp.concatenate([rest, before], axis=0), jnp.concatenate([before, rest], axis=0)
    )
    return jnp.where(at_exit, other + scaled(other_total, whole), whole)


def rms_scale(values, gain):
    return values * lax.rsqrt(jnp.mean(values * values, axis=-1, keepdims=True) + epsilon) * gain


def section_one(projected, rim_rows, conv_weight, conv_bias, step_bias, log_rate):
    tokens = projected.shape[0]
    conv_input = projected[:, :XBC]
    step_raw = projected[:, XBC:]
    extended = jnp.concatenate([rim_rows, conv_input], axis=0)
    conv_sum = conv_bias + conv_weight[0] * extended[0:tokens]
    for offset in range(1, CONV):
        conv_sum = conv_sum + conv_weight[offset] * extended[offset : offset + tokens]
    conv_act = jax.nn.silu(conv_sum)
    blocks = 1
    head_input = conv_act[:, :DI].reshape(blocks, tokens, H, P_SIZE)
    in_coeff = conv_act[:, DI : DI + N].reshape(blocks, tokens, N)
    out_coeff = conv_act[:, DI + N :].reshape(blocks, tokens, N)
    step_size = jax.nn.softplus(step_raw + step_bias).reshape(blocks, tokens, H)
    decays = -jnp.exp(log_rate) * step_size
    inside = jnp.cumsum(decays, axis=1)
    inside_heads = jnp.swapaxes(inside, 1, 2)
    step_heads = jnp.swapaxes(step_size, 1, 2)
    scores = jnp.einsum("ktn,ksn->kts", out_coeff, in_coeff, precision=highest)
    log_gaps = inside_heads[:, :, :, None] - inside_heads[:, :, None, :]
    causal = jnp.arange(tokens)[:, None] >= jnp.arange(tokens)[None, :]
    decay_mat = jnp.exp(jnp.where(causal[None, None], log_gaps, -jnp.inf))
    decay_mat = decay_mat * scores[:, None] * step_heads[:, :, None, :]
    inner_out = jnp.einsum("khts,kshp->kthp", decay_mat, head_input, precision=highest)
    last_log = inside[:, -1:, :]
    tail_weight = jnp.exp(last_log - inside) * step_size
    span_state = jnp.einsum(
        "ksh,kshp,ksn->khpn", tail_weight, head_input, in_coeff, precision=highest
    )

    final_state = span_state[0]
    cumulative = inside.reshape(tokens, H)
    ssm_zero = inner_out.reshape(tokens, H, P_SIZE)
    return (
        ssm_zero,
        cumulative,
        out_coeff.reshape(tokens, N),
        head_input.reshape(tokens, H, P_SIZE),
        final_state,
    )


def section_two(
    gate_part, ssm_zero, cumulative, out_coeff, head_input, state_in, skip_gain, gate_gain
):
    tokens = gate_part.shape[0]
    entering = jnp.einsum("tn,hpn->thp", out_coeff, state_in, precision=highest)
    ssm_full = (
        ssm_zero
        + jnp.exp(cumulative)[:, :, None] * entering
        + skip_gain[None, :, None] * head_input
    )
    gated = ssm_full.reshape(tokens, DI) * jax.nn.silu(gate_part)
    return rms_scale(gated, gate_gain)


def by_owner(rows, columns):
    return jnp.einsum("ftk,ftc->kc", rows, columns, preferred_element_type=jnp.float32)


def on_device(
    inputs,
    cotangent,
    inproj,
    outproj,
    norm_gain,
    gate_gain,
    conv_weight,
    conv_bias,
    step_bias,
    log_rate,
    skip_gain,
):
    stream = inputs[0].astype(jnp.float32)
    tokens = stream.shape[0]
    rim = CONV - 1
    rim_start = tokens - rim
    index, shard = lax.axis_index("seq"), lax.axis_index("fsdp")
    rest_full = lax.all_gather(inproj[0, :, DI:], "fsdp", axis=0, tiled=True)
    halo = passed_along(inputs[0, rim_start:], "seq", 1).astype(jnp.float32)
    normed_f, pull_norm = jax.vjp(rms_scale, stream, norm_gain[0])
    normed = normed_f.astype(jnp.bfloat16)
    halo_normed = rms_scale(halo, norm_gain[0]).astype(jnp.bfloat16)
    extra = jnp.pad(halo_normed, ((0, 8 - rim), (0, 0)))
    both = jnp.dot(
        jnp.concatenate([normed, extra], axis=0), rest_full, preferred_element_type=jnp.float32
    )
    projected = both[:tokens]
    rim_rows = both[tokens : tokens + rim, :XBC]
    gate_full = lax.all_gather(inproj[0, :, :DI], "fsdp", axis=0, tiled=True)
    out_rows = outproj.shape[1]
    mixture = lax.all_gather(
        jnp.concatenate([outproj[0], cotangent[0], normed], axis=0), "fsdp"
    )
    outproj_full = mixture[:, :out_rows].reshape(-1, outproj.shape[2])
    outer_all = mixture[:, out_rows : out_rows + tokens]
    normed_own = lax.dynamic_slice_in_dim(
        mixture[:, out_rows + tokens :], shard * inproj.shape[1], inproj.shape[1], 2
    )
    projected_gate = jnp.dot(normed, gate_full, preferred_element_type=jnp.float32)
    first_out, pull_first = jax.vjp(
        section_one, projected, rim_rows, conv_weight[0], conv_bias[0], step_bias[0], log_rate[0]
    )
    ssm_zero, cumulative, out_coeff, head_input, final_state = first_out
    total_log = cumulative[tokens - 1]
    state_in = handed_on(final_state, total_log, "seq", 1)
    mixed_f, pull_second = jax.vjp(
        section_two,
        projected_gate,
        ssm_zero,
        cumulative,
        out_coeff,
        head_input,
        state_in,
        skip_gain[0],
        gate_gain[0],
    )
    mixed_out = mixed_f.astype(jnp.bfloat16)
    output = stream + jnp.dot(mixed_out, outproj_full, preferred_element_type=jnp.float32)
    out_grad = cotangent[0]
    mix_grad = jnp.dot(out_grad, outproj_full.T, preferred_element_type=jnp.float32)
    (
        gate_grad,
        zero_grad,
        cum_part,
        coeff_grad,
        head_grad,
        state_grad,
        skip_part,
        gate_part,
    ) = pull_second(mix_grad)
    later_grad = handed_on(state_grad, total_log, "seq", -1)
    mixed_all = lax.all_gather(mixed_out.T, "fsdp")
    mixed_own = lax.dynamic_slice_in_dim(mixed_all, shard * out_rows, out_rows, 1)
    gate_grad_b = gate_grad.astype(jnp.bfloat16)
    gate_all = lax.all_gather(gate_grad_b, "fsdp")
    outproj_term = jnp.einsum(
        "fkt,ftc->kc", mixed_own, outer_all, preferred_element_type=jnp.float32
    ).astype(jnp.bfloat16)
    gate_term = by_owner(normed_own, gate_all).astype(jnp.bfloat16)
    outproj_sum, gate_sum = lax.psum((outproj_term, gate_term), "seq")
    later_grad, outproj_term, gate_term = lax.optimization_barrier(
        (later_grad, outproj_term, gate_term)
    )
    total_grad = jnp.sum(later_grad * state_in, axis=(1, 2)) * jnp.exp(total_log)
    cum_grad = cum_part + jnp.pad(total_grad[None], ((tokens - 1, 0), (0, 0)))
    proj_first, rim_grad, kernel_part, bias_part, step_part, rate_part = pull_first(
        (zero_grad, cum_grad, coeff_grad, head_grad, later_grad)
    )
    rim_back = passed_along(rim_grad, "seq", -1)
    rest_grad = proj_first + jnp.pad(
        rim_back, ((rim_start, 0), (0, projected.shape[1] - XBC))
    )
    rest_grad_b = rest_grad.astype(jnp.bfloat16)
    owners, rest_parts = [0], [rest_grad_b]
    bit = lax.axis_size("fsdp") // 2
    while bit > 0:
        pairs = [(i, i ^ bit) for i in range(lax.axis_size("fsdp"))]
        rest_parts += [lax.ppermute(part, "fsdp", pairs) for part in rest_parts]
        owners += [owner ^ bit for owner in owners]
        bit //= 2
    contract = (((1,), (1,)), ((), ()))
    normed_grad = lax.dot_general(
        gate_grad_b, gate_full, contract, preferred_element_type=jnp.float32
    ) + lax.dot_general(rest_grad_b, rest_full, contract, preferred_element_type=jnp.float32)
    stream_part, norm_part = pull_norm(normed_grad)
    grad_stream = cotangent[0].astype(jnp.float32) + stream_part
    in_rows = inproj.shape[1]
    width = rest_grad_b.shape[1]
    small = [norm_part, gate_part, kernel_part, bias_part, step_part, rate_part, skip_part]
    sizes = [part.size for part in small]
    total = sum(sizes)
    rows = -(-total // width)
    lines = -(-total // 1024) * 8
    flat = jnp.concatenate([part.reshape(-1) for part in small] + [jnp.zeros((lines * 128 - total,), jnp.float32)])
    group = jnp.sum(lax.all_gather(flat.reshape(lines, 128), "fsdp"), axis=0).reshape(-1)
    group = jnp.pad(group[:total], (0, rows * width - total)).reshape(rows, width)
    rest_term = sum(
        lax.dot_general(
            lax.dynamic_index_in_dim(normed_own, shard ^ owner, 0, keepdims=False),
            part,
            (((0,), (0,)), ((), ())),
            preferred_element_type=jnp.float32,
        )
        for owner, part in zip(owners, rest_parts)
    )
    joined = jnp.concatenate([rest_term, group], axis=0).astype(jnp.bfloat16)
    joined, outproj_sum, gate_sum = lax.optimization_barrier((joined, outproj_sum, gate_sum))
    joined_sum = lax.psum(joined, "seq")
    inproj_grad = jnp.concatenate([gate_sum, joined_sum[:in_rows]], axis=1).astype(jnp.float32)
    flat = joined_sum[in_rows:].astype(jnp.float32).reshape(-1)
    outs, at = [], 0
    for part, size in zip(small, sizes):
        outs.append(flat[at : at + size].reshape((1,) + part.shape))
        at += size
    return (
        output.astype(jnp.bfloat16)[None],
        grad_stream.astype(jnp.bfloat16)[None],
        inproj_grad[None],
        outproj_sum.astype(jnp.float32)[None],
        *outs,
    )


def solution(mesh):
    placed = (
        P("fsdp", "seq", None),
        P("fsdp", "seq", None),
        P(None, "fsdp", None),
        P(None, "fsdp", None),
        P(),
        P(),
        P(),
        P(),
        P(),
        P(),
        P(),
    )
    return jax.shard_map(
        on_device,
        mesh=mesh,
        in_specs=placed,
        out_specs=(
            P("fsdp", "seq", None),
            P("fsdp", "seq", None),
            P(None, "fsdp", None),
            P(None, "fsdp", None),
            P(),
            P(),
            P(),
            P(),
            P(),
            P(),
            P(),
        ),
        check_vma=False,
    )
```
